32 devices in a mesh: img: 8 (over z, x), head: 4 (over y, core).
Axes of the slice: x: 2, y: 2, z: 4, core: 2. Of those that a mesh axis runs over, the one named last changes fastest.
Arguments:
- inputs: bfloat16 [2048, 1280], P('img'), may hold values from -6 to 6
- middle: bfloat16 [2048, 1280], P('img'), may hold values from -6 to 6
- out_grad: bfloat16 [2048, 1280], P('img'), may hold values from -6 to 6
- cached_maps: bfloat16 [8, 16, 256, 256], P('img', 'head'), may hold values from 0 to 1, as said below
- w_value: bfloat16 [1280, 1280], P(None, 'head'), may hold values from -0.15625 to 0.15625
- w_out: bfloat16 [1280, 1280], P('head'), may hold values from -0.15625 to 0.15625
- w_up: bfloat16 [1280, 2560], P(None, 'head'), may hold values from -0.15625 to 0.15625
- w_down: bfloat16 [2560, 1280], P('head'), may hold values from -0.125 to 0.125
Outputs:
- in_grad: bfloat16 [2048, 1280], P(('img', 'head'))
- grad_value: float32 [1280, 1280], P('img', 'head')
- grad_out: float32 [1280, 1280], P('head', 'img')
- grad_up: float32 [1280, 2560], P('img', 'head')
- grad_down: float32 [2560, 1280], P('head', 'img')
The draws below stay inside these ranges and needn't reach their ends.
Inputs may be any that keep to these rules, and one draw needn't show every extreme that they name: `cached_maps`: every row of every map is positive and sums to one up to rounding.
All inputs are finite; a program needn't handle non-finite values.
Results may differ from the reference program's by a relative error of at most 0.0069.
Values may be sent and summed in bfloat16 or wider, within the bound.
A program may use at most 128 MiB of HBM per device.

```python
import jax
import jax.numpy as jnp
from jax import lax

D = 1280
FF = 2560
HEADS = 16
TOK = 256
HDIM = 80
IMAGES = 8


def draw_cached_maps(key, part):
    first_key, second_key = jax.random.split(jax.random.fold_in(key, 7))
    sharpness = jnp.exp(jax.random.uniform(first_key, (IMAGES, HEADS, 1, 1), jnp.float32, -0.7, 1.4))
    logits = jax.random.normal(second_key, (IMAGES, HEADS, TOK, TOK), jnp.float32)
    return jax.nn.softmax(logits * sharpness, axis=-1).astype(jnp.bfloat16)


def strengthened(array, rng, source, target, parts, factor):
    owner, partner = [(jnp.arange(array.shape[axis_at]) // (array.shape[axis_at] // parts)).reshape([-1 if axis == axis_at else 1 for axis in range(array.ndim)]) for axis_at in (source, target)]
    chosen = jax.random.permutation(rng, parts)[partner]
    strong = (owner == chosen) | (owner == (partner + parts // 2) % parts)
    return jnp.where(strong, factor * array, array)


def steps_of(own_key, extent, pieces, low, top_value):
    def one(position, blocks):
        steps = jax.random.uniform(jax.random.fold_in(jax.random.fold_in(own_key, 6), position), (blocks,), jnp.float32, low / len(pieces), top_value / len(pieces))
        return jnp.repeat(jnp.exp(steps), extent[position] // blocks).reshape((-1,) + (1,) * (len(extent) - position - 1))

    level = one(*pieces[0])
    for cut in pieces[1:]:
        level = level * one(*cut)
    return level


def noise(own_key, dims, width, bound, pieces=(), kind=jnp.bfloat16):
    values = width * jax.random.normal(own_key, dims, jnp.float32)
    if pieces:
        values = values * steps_of(own_key, dims, pieces, -0.22, 0.18)
    return jnp.clip(values, -bound, bound).astype(kind)


def noise_with(stream_key, extent, scale, reach, cuts, heavy, dtype=jnp.bfloat16):
    drawn = scale * jax.random.normal(stream_key, extent, jnp.float32)
    if cuts:
        drawn = drawn * steps_of(stream_key, extent, cuts, -0.22, 0.18)
    return jnp.clip(strengthened(drawn, jax.random.fold_in(stream_key, 3), *heavy), -reach, reach).astype(dtype)


def setup_inputs(seed: int = 0) -> dict:
    key_of = jax.random.split(jax.random.key(seed), 9)
    inputs = noise_with(key_of[0], (IMAGES * TOK, D), 1.0, 6.0, ((0, 8),), (0, 1, 8, 2.0))
    middle = noise_with(key_of[1], (IMAGES * TOK, D), 1.0, 6.0, ((0, 8),), (0, 1, 8, 2.0))
    out_grad = noise_with(key_of[2], (IMAGES * TOK, D), 1.0, 6.0, ((0, 8),), (0, 1, 8, 2.0))
    cached_maps = draw_cached_maps(jax.random.fold_in(key_of[8], 71), 0)
    w_value = noise(key_of[4], (D, D), D ** -0.5, 0.15625, ((1, 4),))
    w_out = noise(key_of[5], (D, D), D ** -0.5, 0.15625, ((0, 4),))
    w_up = noise(key_of[6], (D, FF), D ** -0.5, 0.15625, ((1, 4),))
    w_down = noise(key_of[7], (FF, D), FF ** -0.5, 0.125, ((0, 4),))
    return {"inputs": inputs, "middle": middle, "out_grad": out_grad, "cached_maps": cached_maps, "w_value": w_value, "w_out": w_out, "w_up": w_up, "w_down": w_down}


def norm_rows(rows):
    centre = rows - lax.optimization_barrier(jnp.mean(rows, axis=-1, keepdims=True))
    spread = lax.optimization_barrier(jnp.mean(centre * centre, axis=-1, keepdims=True))
    return centre * lax.rsqrt(spread + 1e-06)

def norm_back(rows, grad):
    centre = rows - lax.optimization_barrier(jnp.mean(rows, axis=-1, keepdims=True))
    factor = lax.rsqrt(lax.optimization_barrier(jnp.mean(centre * centre, axis=-1, keepdims=True)) + 1e-06)
    normed = centre * factor
    return factor * (grad - lax.optimization_barrier(jnp.mean(grad, axis=-1, keepdims=True)) - normed * lax.optimization_barrier(jnp.mean(grad * normed, axis=-1, keepdims=True)))

def gelu_tanh(pre):
    return jax.nn.gelu(pre, approximate=True)

def reference(inputs, middle, out_grad, cached_maps, w_value, w_out, w_up, w_down):
    inputs_all = inputs.reshape(IMAGES, TOK, D)
    middle_all = middle.reshape(IMAGES, TOK, D)
    grads_all = out_grad.reshape(IMAGES, TOK, D)

    def one_image(totals, item):
        source, saved, upstream, maps_one = item
        source_f = source.astype(jnp.float32)
        saved_f = saved.astype(jnp.float32)
        normed_in = norm_rows(source_f).astype(jnp.bfloat16)
        values = jnp.dot(normed_in, w_value, preferred_element_type=jnp.float32).astype(jnp.bfloat16)
        maps_f = maps_one.astype(jnp.float32)
        attended = jnp.einsum('htk,khd->thd', maps_f, values.reshape(TOK, HEADS, HDIM).astype(jnp.float32))
        attended = attended.astype(jnp.bfloat16).reshape(TOK, D)
        normed_mid = norm_rows(saved_f).astype(jnp.bfloat16)
        pre = jnp.dot(normed_mid, w_up, preferred_element_type=jnp.float32)
        hidden = gelu_tanh(pre).astype(jnp.bfloat16)
        hidden_grad = jnp.dot(upstream, w_down.T, preferred_element_type=jnp.float32)
        pre_grad = jax.vjp(gelu_tanh, pre)[1](hidden_grad)[0].astype(jnp.bfloat16)
        grad_down = jnp.dot(hidden.T, upstream, preferred_element_type=jnp.float32)
        grad_up = jnp.dot(normed_mid.T, pre_grad, preferred_element_type=jnp.float32)
        mid_grad = upstream.astype(jnp.float32) + norm_back(saved_f, jnp.dot(pre_grad, w_up.T, preferred_element_type=jnp.float32))
        mid_grad_b = mid_grad.astype(jnp.bfloat16)
        grad_out = jnp.dot(attended.T, mid_grad_b, preferred_element_type=jnp.float32)
        att_grad = jnp.dot(mid_grad_b, w_out.T, preferred_element_type=jnp.float32).astype(jnp.bfloat16)
        value_grad = jnp.einsum('htk,thd->khd', maps_f, att_grad.reshape(TOK, HEADS, HDIM).astype(jnp.float32))
        value_grad = value_grad.astype(jnp.bfloat16).reshape(TOK, D)
        grad_value = jnp.dot(normed_in.T, value_grad, preferred_element_type=jnp.float32)
        in_grad = mid_grad + norm_back(source_f, jnp.dot(value_grad, w_value.T, preferred_element_type=jnp.float32))
        totals = (totals[0] + grad_value, totals[1] + grad_out, totals[2] + grad_up, totals[3] + grad_down)
        return (totals, in_grad.astype(jnp.bfloat16))
    start = (jnp.zeros((D, D), jnp.float32), jnp.zeros((D, D), jnp.float32), jnp.zeros((D, FF), jnp.float32), jnp.zeros((FF, D), jnp.float32))
    totals, in_grads = lax.scan(one_image, start, (inputs_all, middle_all, grads_all, cached_maps))
    return (in_grads.reshape(IMAGES * TOK, D), totals[0], totals[1], totals[2], totals[3])
```

```python
import jax
import jax.numpy as jnp
from jax import lax
from jax.experimental import pallas as pl
from jax.experimental.pallas import tpu as pltpu
from jax.sharding import PartitionSpec as P


def norm_rows(rows):
    centre = rows - jnp.mean(rows, axis=-1, keepdims=True)
    spread = jnp.mean(centre * centre, axis=-1, keepdims=True)
    return centre * lax.rsqrt(spread + 1e-06)


def norm_back(rows, grad):
    centre = rows - jnp.mean(rows, axis=-1, keepdims=True)
    factor = lax.rsqrt(jnp.mean(centre * centre, axis=-1, keepdims=True) + 1e-06)
    normed = centre * factor
    return factor * (
        grad
        - jnp.mean(grad, axis=-1, keepdims=True)
        - normed * jnp.mean(grad * normed, axis=-1, keepdims=True)
    )


def gelu_tanh(pre):
    return jax.nn.gelu(pre, approximate=True)


def on_device(inputs, middle, out_grad, cached_maps, w_value, w_out, w_up, w_down):
    tok_rows = inputs.shape[0]
    heads_here = cached_maps.shape[1]
    share = tok_rows // lax.axis_size("head")
    first = lax.axis_index("head") * share
    maps_here = cached_maps[0]
    normed_in = norm_rows(inputs.astype(jnp.float32)).astype(jnp.bfloat16)
    values = jnp.dot(normed_in, w_value, preferred_element_type=jnp.float32).astype(jnp.bfloat16)
    head_size = values.shape[1] // heads_here
    attended = jnp.einsum(
        "htk,khd->thd",
        maps_here,
        values.reshape(tok_rows, heads_here, head_size),
        preferred_element_type=jnp.float32,
    )
    attended = attended.astype(jnp.bfloat16).reshape(tok_rows, -1)
    middle_f = middle.astype(jnp.float32)
    normed_mid = norm_rows(middle_f).astype(jnp.bfloat16)
    pre = jnp.dot(normed_mid, w_up, preferred_element_type=jnp.float32)
    hidden = gelu_tanh(pre).astype(jnp.bfloat16)
    hidden_grad = jnp.einsum("td,fd->tf", out_grad, w_down, preferred_element_type=jnp.float32)
    pre_grad = jax.vjp(gelu_tanh, pre)[1](hidden_grad)[0].astype(jnp.bfloat16)
    down_term = jnp.einsum("tf,td->fd", hidden, out_grad, preferred_element_type=jnp.float32)
    mid_part = jnp.einsum("tf,df->td", pre_grad, w_up, preferred_element_type=jnp.float32)
    out_rows = lax.dynamic_slice_in_dim(out_grad, first, share, 0).astype(jnp.float32)
    mid_share = lax.psum_scatter(mid_part, "head", scatter_dimension=0, tiled=True)
    mid_own = out_rows + norm_back(lax.dynamic_slice_in_dim(middle_f, first, share, 0), mid_share)
    mid_grad_b = lax.all_gather(mid_own.astype(jnp.bfloat16), "head", axis=0, tiled=True)
    outproj_term = jnp.einsum("te,td->ed", attended, mid_grad_b, preferred_element_type=jnp.float32)
    att_grad = jnp.einsum(
        "td,ed->te", mid_grad_b, w_out, preferred_element_type=jnp.float32
    ).astype(jnp.bfloat16)
    value_grad = jnp.einsum(
        "htk,thd->khd",
        maps_here,
        att_grad.reshape(tok_rows, heads_here, head_size),
        preferred_element_type=jnp.float32,
    )
    value_grad = value_grad.astype(jnp.bfloat16).reshape(tok_rows, -1)
    input_part = jnp.einsum("te,de->td", value_grad, w_value, preferred_element_type=jnp.float32)
    inputs_own = lax.dynamic_slice_in_dim(inputs, first, share, 0).astype(jnp.float32)
    input_share = lax.psum_scatter(input_part, "head", scatter_dimension=0, tiled=True)
    in_grad = (mid_own + norm_back(inputs_own, input_share)).astype(jnp.bfloat16)
    picked = normed_mid
    up_term = jnp.einsum("tr,tf->rf", picked, pre_grad, preferred_element_type=jnp.float32)
    picked = normed_in
    value_term = jnp.einsum("tr,te->re", picked, value_grad, preferred_element_type=jnp.float32)
    grad_down, grad_out = (
        lax.psum_scatter(down_term, "img", scatter_dimension=1, tiled=True),
        lax.psum_scatter(outproj_term, "img", scatter_dimension=1, tiled=True),
    )
    grad_up, grad_value = (
        lax.psum_scatter(up_term, "img", scatter_dimension=0, tiled=True),
        lax.psum_scatter(value_term, "img", scatter_dimension=0, tiled=True),
    )
    return (in_grad, grad_value, grad_out, grad_up, grad_down)


MESH = pl.DeviceIdType.MESH
F32 = jnp.float32
BF16 = jnp.bfloat16
COPIES = 64
GELU_C = 0.7978845608028654


def dot_nn(a, b):
    return lax.dot_general(a, b, (((1,), (0,)), ((), ())), preferred_element_type=F32)


def dot_nt(a, b):
    return lax.dot_general(a, b, (((1,), (1,)), ((), ())), preferred_element_type=F32)


def dot_tn(a, b):
    return lax.dot_general(a, b, (((0,), (0,)), ((), ())), preferred_element_type=F32)


def gelu_and_slope(pre):
    square = pre * pre
    tanh = jnp.tanh(GELU_C * pre * (1.0 + 0.044715 * square))
    half = 0.5 * (1.0 + tanh)
    slope = half + 0.5 * pre * (1.0 - tanh * tanh) * (GELU_C * (1.0 + 3 * 0.044715 * square))
    return pre * half, slope


def block_kernel(
    inputs_h, middle_h, out_grad_h, maps_h, w_value_h, w_out_h, w_up_h, w_down_h,
    in_grad, mlp_sum, att_sum,
    inputs, middle, maps, w_value_t, w_out, w_up, w_down,
    og, nm, ogt, nmt, hid, prg, mlp_part, mlp_send, mlp_recv,
    mp1, ra1, sb1, rb1, mp2, ra2, sb2, rb2, mid_rows, midb,
    nint, nint_p, midbt, midbt_p, attd, attd_p, vgr, vgr_p,
    go_part, go_send, go_recv, go_pass, go_last, gv_part, gv_send, gv_recv, gv_pass, gv_last,
    local_sem, send_sem, recv_sem,
):
    tok, width = inputs.shape
    share = tok // 4
    heads_here = maps.shape[0]
    local = attd.shape[1]
    hdim = local // heads_here
    ff = w_up.shape[1]
    piece = mlp_sum.shape[0]
    img = lax.axis_index("img")
    head = lax.axis_index("head")
    z, x = img // 2, img % 2
    y, c = head // 2, head % 2
    upper, parity = z // 2, z % 2
    x_peer = {"img": z * 2 + (1 - x)}
    side_peer = {"img": (upper * 2 + 1 - parity) * 2 + x}
    cross_peer = {"img": ((1 - upper) * 2 + parity) * 2 + x}
    y_peer = {"head": (1 - y) * 2 + c}
    core_peer = {"head": y * 2 + (1 - c)}
    used = []

    def copy(src, dst, peer):
        sem = len(used)
        used.append(sem)
        return pltpu.make_async_remote_copy(
            src_ref=src, dst_ref=dst, send_sem=send_sem.at[sem], recv_sem=recv_sem.at[sem],
            device_id=peer, device_id_type=MESH,
        )

    started = []

    def send(src, dst, peer):
        one = copy(src, dst, peer)
        one.start()
        started.append(one)
        return one

    def quarter(h):
        return pl.ds(pl.multiple_of(h * share, share), share)

    mine, theirs = quarter(head), quarter((1 - y) * 2 + c)

    barrier = pltpu.get_barrier_semaphore()
    for peer in (x_peer, side_peer, cross_peer, y_peer, core_peer):
        pl.semaphore_signal(barrier, inc=1, device_id=peer, device_id_type=MESH)
    loads = [
        pltpu.make_async_copy(src, dst, local_sem.at[i])
        for i, (src, dst) in enumerate([
            (middle_h, middle), (out_grad_h, og.at[0]), (w_up_h, w_up), (w_down_h, w_down),
            (inputs_h, inputs), (w_value_h, w_value_t), (maps_h, maps), (w_out_h, w_out),
        ])
    ]
    for one in loads:
        one.start()
    loads[0].wait()
    nm[0] = norm_rows(middle[...].astype(F32)).astype(BF16)
    loads[1].wait()
    pl.semaphore_wait(barrier, 5)
    raw = (og, nm)
    slot1 = [send(a.at[0, mine], a.at[1, mine], side_peer) for a in raw]
    slot2 = [send(a.at[0, mine], a.at[2, mine], cross_peer) for a in raw]

    window = pl.ds(pl.multiple_of(upper * (width // 2) + parity * 256, 128), 384)

    def expand(s):
        rows = pl.ds(s * tok, tok)
        value, slope = gelu_and_slope(dot_nn(nm[s], w_up[...]))
        hid[rows] = value.astype(BF16)
        prg[rows] = (slope * dot_nt(og[s], w_down[...])).astype(BF16)

    def turn(s):
        rows = pl.ds(s * tok, tok)
        ogt[:, rows] = og[s, :, window].T
        nmt[:, rows] = nm[s, :, window].T

    def spread_y(s):
        return [send(a.at[s, mine], a.at[s, mine], y_peer) for a in raw]

    def spread_core(s, rows):
        return [send(a.at[s, rows], a.at[s, rows], core_peer) for a in raw]

    def take(copies):
        for one in copies:
            one.wait_recv()

    loads[2].wait()
    loads[3].wait()
    expand(0)
    part = dot_nt(prg[0:tok], w_up[...]).astype(BF16)
    for q in range(4):
        mp1[q % 2, q // 2] = part[q * share:(q + 1) * share]
    core1 = send(mp1.at[1 - c], ra1, core_peer)

    for one in loads[4:]:
        one.wait()
    normed_in = norm_rows(inputs[...].astype(F32)).astype(BF16)
    values = dot_nt(normed_in, w_value_t[...]).astype(BF16)

    core1.wait_recv()
    sb1[...] = (mp1[c].astype(F32) + ra1[...].astype(F32)).astype(BF16)
    y1 = send(sb1, rb1, y_peer)

    column = lax.broadcasted_iota(jnp.int32, (tok, local), 1)

    def own_columns(array, h):
        keep = (column >= h * hdim) & (column < (h + 1) * hdim)
        return jnp.where(keep, array, jnp.zeros_like(array))

    total = dot_nn(maps[0], own_columns(values, 0))
    for h in range(1, heads_here):
        total = total + dot_nn(maps[h], own_columns(values, h))
    attd[...] = total.astype(BF16)
    att_x = send(attd, attd_p, x_peer)

    def halves(array, ref):
        turned = array.T
        for i in range(8):
            ref[i % 2, i // 2] = turned[i * piece:(i + 1) * piece]

    pair = pl.ds(c * 2, 2)
    halves(normed_in, nint)
    nint_x = send(nint.at[1 - x, pair], nint_p.at[pair], x_peer)
    turn(0)

    take(slot1)
    slot1_y = spread_y(1)
    slot1_core = spread_core(1, mine)
    nint_x.wait_recv()
    nint_core = send(nint_p.at[pair], nint_p.at[pair], core_peer)

    y1.wait_recv()
    mid_core = []
    for b in range(2):
        rows = quarter(b * 2 + c)
        grad = mp1[c, b].astype(F32) + ra1[b].astype(F32) + rb1[b].astype(F32)
        own = og[0, rows].astype(F32) + norm_back(middle[rows].astype(F32), grad)
        mid_rows[b] = own
        midb[rows] = own.astype(BF16)
        mid_core.append(send(midb.at[rows], midb.at[rows], core_peer))
    take(slot2)
    slot3 = [send(a.at[2, mine], a.at[3, mine], side_peer) for a in raw]
    slot2_core = spread_core(2, mine)
    take(mid_core)
    halves(midb[...], midbt)
    midbt_x = send(midbt.at[1 - x, pair], midbt_p.at[pair], x_peer)
    att_grad = dot_nt(midb[...], w_out[...]).astype(BF16)
    total = dot_tn(maps[0], own_columns(att_grad, 0))
    for h in range(1, heads_here):
        total = total + dot_tn(maps[h], own_columns(att_grad, h))
    vgr[...] = total.astype(BF16)
    vgr_x = send(vgr, vgr_p, x_peer)
    slot2_y = spread_y(2)
    part = dot_nn(vgr[...], w_value_t[...]).astype(BF16)
    for q in range(4):
        mp2[q % 2, q // 2] = part[q * share:(q + 1) * share]
    core2 = send(mp2.at[1 - c], ra2, core_peer)
    take(slot1_y)
    slot1_core += spread_core(1, theirs)

    midbt_x.wait_recv()
    midbt_core = send(midbt_p.at[pair], midbt_p.at[pair], core_peer)
    take(slot1_core)
    expand(1)
    turn(1)
    core2.wait_recv()
    sb2[...] = (mp2[c, 1 - y].astype(F32) + ra2[1 - y].astype(F32)).astype(BF16)
    y2 = send(sb2, rb2, y_peer)

    def products(left, left_p, right, right_p, part_ref, send_ref):
        flat = 4 * piece
        total = dot_nn(left[x].reshape(flat, tok), right[...])
        total = total + dot_nn(left_p[...].reshape(flat, tok), right_p[...])
        for i in range(4):
            one = total[i * piece:(i + 1) * piece]
            part_ref[i % 2, i // 2] = one
            send_ref[i % 2, i // 2] = one.astype(BF16)

    att_x.wait_recv()
    midbt_core.wait_recv()
    products(midbt, midbt_p, attd, attd_p, go_part, go_send)
    go_side = send(go_send.at[1 - parity], go_recv, side_peer)
    nint_core.wait_recv()
    vgr_x.wait_recv()
    products(nint, nint_p, vgr, vgr_p, gv_part, gv_send)
    gv_side = send(gv_send.at[1 - parity], gv_recv, side_peer)

    take(slot3)
    slot3_y = spread_y(3)
    slot3_core = spread_core(3, mine)
    take(slot2_y)
    slot2_core += spread_core(2, theirs)
    take(slot2_core)
    expand(2)
    turn(2)

    def halve(side, part_ref, recv, pass_ref, last):
        side.wait_recv()
        other = 1 - upper
        pass_ref[...] = (part_ref[parity, other] + recv[other].astype(F32)).astype(BF16)
        return send(pass_ref, last, cross_peer)

    go_cross = halve(go_side, go_part, go_recv, go_pass, go_last)
    gv_cross = halve(gv_side, gv_part, gv_recv, gv_pass, gv_last)

    span = 2 * piece
    rows = pl.ds(pl.multiple_of(parity * 64, 64), span)
    done = slice(0, 3 * tok)
    for i, (left, right) in enumerate(((ogt, hid), (nmt, prg))):
        mlp_part[:, i * ff:(i + 1) * ff] = dot_nn(left[rows, done], right[done])
    y2.wait_recv()
    grad = mp2[c, y].astype(F32) + ra2[y].astype(F32) + rb2[...].astype(F32)
    in_grad[...] = (mid_rows[y] + norm_back(inputs[mine].astype(F32), grad)).astype(BF16)
    take(slot3_y)
    slot3_core += spread_core(3, theirs)
    take(slot3_core)
    expand(3)
    turn(3)
    last = slice(3 * tok, 4 * tok)
    mirror = []
    for i, (left, right) in enumerate(((ogt, hid), (nmt, prg))):
        both = mlp_part[:, i * ff:(i + 1) * ff] + dot_nn(left[rows, last], right[last])
        mlp_part[:, i * ff:(i + 1) * ff] = both
        mlp_send[i, 0] = both[0:piece].astype(BF16)
        mlp_send[i, 1] = both[piece:span].astype(BF16)
        mirror.append(send(mlp_send.at[i, 1 - x], mlp_recv.at[i], x_peer))
    go_cross.wait_recv()
    att_sum[:, 0:local] = go_part[parity, upper] + go_recv[upper].astype(F32) + go_last[...].astype(F32)
    gv_cross.wait_recv()
    att_sum[:, local:2 * local] = gv_part[parity, upper] + gv_recv[upper].astype(F32) + gv_last[...].astype(F32)
    own = pl.ds(pl.multiple_of(x * piece, piece), piece)
    for i in range(2):
        mirror[i].wait_recv()
        mlp_sum[:, i * ff:(i + 1) * ff] = mlp_part[own, i * ff:(i + 1) * ff] + mlp_recv[i].astype(F32)
    for one in started:
        one.wait_send()


def split_kernel(in_grad, mlp_sum, att_sum, in_grad_out, value_rows, out_rows_t, up_rows, down_rows_t):
    local, ff = value_rows.shape[1], up_rows.shape[1]
    in_grad_out[...] = in_grad[...]
    down_rows_t[...] = mlp_sum[:, 0:ff]
    up_rows[...] = mlp_sum[:, ff:2 * ff]
    out_rows_t[...] = att_sum[:, 0:local]
    value_rows[...] = att_sum[:, local:2 * local]


def on_device_fused(inputs, middle, out_grad, cached_maps, w_value, w_out, w_up, w_down):
    tok, width = inputs.shape
    local, ff = w_value.shape[1], w_up.shape[1]
    heads_here = cached_maps.shape[1]
    piece = width // lax.axis_size("img")
    share = tok // 4
    vmem = pl.BlockSpec(memory_space=pltpu.VMEM)
    shape = jax.ShapeDtypeStruct
    sums = pl.pallas_call(
        block_kernel,
        out_shape=(
            shape((share, width), BF16),
            shape((piece, 2 * ff), F32),
            shape((piece, 2 * local), F32),
        ),
        in_specs=[pl.BlockSpec(memory_space=pl.ANY)] * 8,
        out_specs=(vmem,) * 3,
        scratch_shapes=[
            pltpu.VMEM((tok, width), BF16),
            pltpu.VMEM((tok, width), BF16),
            pltpu.VMEM((heads_here, tok, tok), BF16),
            pltpu.VMEM((local, width), BF16),
            pltpu.VMEM((local, width), BF16),
            pltpu.VMEM((width, ff), BF16),
            pltpu.VMEM((ff, width), BF16),
            pltpu.VMEM((4, tok, width), BF16),
            pltpu.VMEM((4, tok, width), BF16),
            pltpu.VMEM((384, 4 * tok), BF16),
            pltpu.VMEM((384, 4 * tok), BF16),
            pltpu.VMEM((4 * tok, ff), BF16),
            pltpu.VMEM((4 * tok, ff), BF16),
            pltpu.VMEM((2 * piece, 2 * ff), F32),
            pltpu.VMEM((2, 2, piece, ff), BF16),
            pltpu.VMEM((2, piece, ff), BF16),
            pltpu.VMEM((2, 2, share, width), BF16),
            pltpu.VMEM((2, share, width), BF16),
            pltpu.VMEM((2, share, width), BF16),
            pltpu.VMEM((2, share, width), BF16),
            pltpu.VMEM((2, 2, share, width), BF16),
            pltpu.VMEM((2, share, width), BF16),
            pltpu.VMEM((share, width), BF16),
            pltpu.VMEM((share, width), BF16),
            pltpu.VMEM((2, share, width), F32),
            pltpu.VMEM((tok, width), BF16),
            pltpu.VMEM((2, 4, piece, tok), BF16),
            pltpu.VMEM((4, piece, tok), BF16),
            pltpu.VMEM((2, 4, piece, tok), BF16),
            pltpu.VMEM((4, piece, tok), BF16),
            pltpu.VMEM((tok, local), BF16),
            pltpu.VMEM((tok, local), BF16),
            pltpu.VMEM((tok, local), BF16),
            pltpu.VMEM((tok, local), BF16),
        ] + [
            pltpu.VMEM((2, 2, piece, local), F32),
            pltpu.VMEM((2, 2, piece, local), BF16),
            pltpu.VMEM((2, piece, local), BF16),
            pltpu.VMEM((piece, local), BF16),
            pltpu.VMEM((piece, local), BF16),
        ] * 2 + [
            pltpu.SemaphoreType.DMA((8,)),
            pltpu.SemaphoreType.DMA((COPIES,)),
            pltpu.SemaphoreType.DMA((COPIES,)),
        ],
        compiler_params=pltpu.CompilerParams(
            collective_id=0, has_side_effects=True, vmem_limit_bytes=56 * 1024 * 1024
        ),
    )(inputs, middle, out_grad, cached_maps[0], w_value.T, w_out, w_up, w_down)
    in_grad, value_rows, out_rows_t, up_rows, down_rows_t = pl.pallas_call(
        split_kernel,
        out_shape=(
            shape((share, width), BF16),
            shape((piece, local), F32),
            shape((piece, local), F32),
            shape((piece, ff), F32),
            shape((piece, ff), F32),
        ),
        in_specs=[vmem] * 3,
        out_specs=(vmem,) * 5,
    )(*sums)
    return in_grad, value_rows, out_rows_t.T, up_rows, down_rows_t.T


def solution(mesh):
    fused = mesh.shape["img"] == 8 and mesh.shape["head"] == 4
    return jax.shard_map(
        on_device_fused if fused else on_device,
        mesh=mesh,
        in_specs=(
            P("img", None),
            P("img", None),
            P("img", None),
            P("img", "head", None, None),
            P(None, "head"),
            P("head", None),
            P(None, "head"),
            P("head", None),
        ),
        out_specs=(
            P(("img", "head"), None),
            P("img", "head"),
            P("head", "img"),
            P("img", "head"),
            P("head", "img"),
        ),
        check_vma=False,
    )
```

```python
import jax
import jax.numpy as jnp
from jax import lax
from jax.experimental import pallas as pl
from jax.experimental.pallas import tpu as pltpu
from jax.sharding import PartitionSpec as P


def norm_rows(rows):
    centre = rows - jnp.mean(rows, axis=-1, keepdims=True)
    spread = jnp.mean(centre * centre, axis=-1, keepdims=True)
    return centre * lax.rsqrt(spread + 1e-06)


def norm_back(rows, grad):
    centre = rows - jnp.mean(rows, axis=-1, keepdims=True)
    factor = lax.rsqrt(jnp.mean(centre * centre, axis=-1, keepdims=True) + 1e-06)
    normed = centre * factor
    return factor * (
        grad
        - jnp.mean(grad, axis=-1, keepdims=True)
        - normed * jnp.mean(grad * normed, axis=-1, keepdims=True)
    )


def gelu_tanh(pre):
    return jax.nn.gelu(pre, approximate=True)


def on_device(inputs, middle, out_grad, cached_maps, w_value, w_out, w_up, w_down):
    tok_rows = inputs.shape[0]
    heads_here = cached_maps.shape[1]
    share = tok_rows // lax.axis_size("head")
    first = lax.axis_index("head") * share
    maps_here = cached_maps[0]
    normed_in = norm_rows(inputs.astype(jnp.float32)).astype(jnp.bfloat16)
    values = jnp.dot(normed_in, w_value, preferred_element_type=jnp.float32).astype(jnp.bfloat16)
    head_size = values.shape[1] // heads_here
    attended = jnp.einsum(
        "htk,khd->thd",
        maps_here,
        values.reshape(tok_rows, heads_here, head_size),
        preferred_element_type=jnp.float32,
    )
    attended = attended.astype(jnp.bfloat16).reshape(tok_rows, -1)
    middle_f = middle.astype(jnp.float32)
    normed_mid = norm_rows(middle_f).astype(jnp.bfloat16)
    pre = jnp.dot(normed_mid, w_up, preferred_element_type=jnp.float32)
    hidden = gelu_tanh(pre).astype(jnp.bfloat16)
    hidden_grad = jnp.einsum("td,fd->tf", out_grad, w_down, preferred_element_type=jnp.float32)
    pre_grad = jax.vjp(gelu_tanh, pre)[1](hidden_grad)[0].astype(jnp.bfloat16)
    down_term = jnp.einsum("tf,td->fd", hidden, out_grad, preferred_element_type=jnp.float32)
    mid_part = jnp.einsum("tf,df->td", pre_grad, w_up, preferred_element_type=jnp.float32)
    out_rows = lax.dynamic_slice_in_dim(out_grad, first, share, 0).astype(jnp.float32)
    mid_share = lax.psum_scatter(mid_part, "head", scatter_dimension=0, tiled=True)
    mid_own = out_rows + norm_back(lax.dynamic_slice_in_dim(middle_f, first, share, 0), mid_share)
    mid_grad_b = lax.all_gather(mid_own.astype(jnp.bfloat16), "head", axis=0, tiled=True)
    outproj_term = jnp.einsum("te,td->ed", attended, mid_grad_b, preferred_element_type=jnp.float32)
    att_grad = jnp.einsum(
        "td,ed->te", mid_grad_b, w_out, preferred_element_type=jnp.float32
    ).astype(jnp.bfloat16)
    value_grad = jnp.einsum(
        "htk,thd->khd",
        maps_here,
        att_grad.reshape(tok_rows, heads_here, head_size),
        preferred_element_type=jnp.float32,
    )
    value_grad = value_grad.astype(jnp.bfloat16).reshape(tok_rows, -1)
    input_part = jnp.einsum("te,de->td", value_grad, w_value, preferred_element_type=jnp.float32)
    inputs_own = lax.dynamic_slice_in_dim(inputs, first, share, 0).astype(jnp.float32)
    input_share = lax.psum_scatter(input_part, "head", scatter_dimension=0, tiled=True)
    in_grad = (mid_own + norm_back(inputs_own, input_share)).astype(jnp.bfloat16)
    picked = normed_mid
    up_term = jnp.einsum("tr,tf->rf", picked, pre_grad, preferred_element_type=jnp.float32)
    picked = normed_in
    value_term = jnp.einsum("tr,te->re", picked, value_grad, preferred_element_type=jnp.float32)
    grad_down, grad_out = (
        lax.psum_scatter(down_term, "img", scatter_dimension=1, tiled=True),
        lax.psum_scatter(outproj_term, "img", scatter_dimension=1, tiled=True),
    )
    grad_up, grad_value = (
        lax.psum_scatter(up_term, "img", scatter_dimension=0, tiled=True),
        lax.psum_scatter(value_term, "img", scatter_dimension=0, tiled=True),
    )
    return (in_grad, grad_value, grad_out, grad_up, grad_down)


MESH = pl.DeviceIdType.MESH
F32 = jnp.float32
BF16 = jnp.bfloat16
COPIES = 64
GELU_C = 0.7978845608028654


def dot_nn(a, b):
    return lax.dot_general(a, b, (((1,), (0,)), ((), ())), preferred_element_type=F32)


def dot_nt(a, b):
    return lax.dot_general(a, b, (((1,), (1,)), ((), ())), preferred_element_type=F32)


def dot_tn(a, b):
    return lax.dot_general(a, b, (((0,), (0,)), ((), ())), preferred_element_type=F32)


def gelu_and_slope(pre):
    square = pre * pre
    tanh = jnp.tanh(GELU_C * pre * (1.0 + 0.044715 * square))
    half = 0.5 * (1.0 + tanh)
    slope = half + 0.5 * pre * (1.0 - tanh * tanh) * (GELU_C * (1.0 + 3 * 0.044715 * square))
    return pre * half, slope


def block_kernel(
    inputs_h, middle_h, out_grad_h, maps_h, w_value_h, w_out_h, w_up_h, w_down_h,
    in_grad, gv_sum, go_sum, up_sum, down_sum,
    inputs, middle, maps, w_value_t, w_out, w_up, w_down,
    og, nm, ogt, nmt, hid, prg, grad_h, mlp_part, mlp_send, mlp_recv,
    mp1, ra1, sb1, rb1, mp2, ra2, sb2, rb2, mid_rows, midb,
    nint, nint_p, midbt, midbt_p, attd, attd_p, vgr, vgr_p,
    go_part, go_send, go_recv, go_pass, go_last, gv_part, gv_send, gv_recv, gv_pass, gv_last,
    local_sem, send_sem, recv_sem,
):
    tok, width = inputs.shape
    share = tok // 4
    heads_here = maps.shape[0]
    local = attd.shape[1]
    hdim = local // heads_here
    ff = w_up.shape[1]
    piece = up_sum.shape[0]
    img = lax.axis_index("img")
    head = lax.axis_index("head")
    z, x = img // 2, img % 2
    y, c = head // 2, head % 2
    upper, parity = z // 2, z % 2
    x_peer = {"img": z * 2 + (1 - x)}
    side_peer = {"img": (upper * 2 + 1 - parity) * 2 + x}
    cross_peer = {"img": ((1 - upper) * 2 + parity) * 2 + x}
    y_peer = {"head": (1 - y) * 2 + c}
    core_peer = {"head": y * 2 + (1 - c)}
    used = []

    def copy(src, dst, peer):
        sem = len(used)
        used.append(sem)
        return pltpu.make_async_remote_copy(
            src_ref=src, dst_ref=dst, send_sem=send_sem.at[sem], recv_sem=recv_sem.at[sem],
            device_id=peer, device_id_type=MESH,
        )

    started = []

    def send(src, dst, peer):
        one = copy(src, dst, peer)
        one.start()
        started.append(one)
        return one

    def quarter(h):
        return pl.ds(pl.multiple_of(h * share, share), share)

    mine, theirs = quarter(head), quarter((1 - y) * 2 + c)

    barrier = pltpu.get_barrier_semaphore()
    for peer in (x_peer, side_peer, cross_peer, y_peer, core_peer):
        pl.semaphore_signal(barrier, inc=1, device_id=peer, device_id_type=MESH)
    loads = [
        pltpu.make_async_copy(src, dst, local_sem.at[i])
        for i, (src, dst) in enumerate([
            (middle_h, middle), (out_grad_h, og.at[0]), (w_up_h, w_up), (w_down_h, w_down),
            (inputs_h, inputs), (w_value_h, w_value_t), (maps_h, maps), (w_out_h, w_out),
        ])
    ]
    for one in loads[:4]:
        one.start()
    loads[0].wait()
    for one in loads[4:]:
        one.start()
    nm[0] = norm_rows(middle[...].astype(F32)).astype(BF16)
    loads[1].wait()
    pl.semaphore_wait(barrier, 5)
    raw = (og, nm)
    direct = ()
    slot1, slot2 = [], []

    def first_send(a):
        slot2.append(send(a.at[0, mine], a.at[2, mine], cross_peer))
        slot1.append([send(a.at[0, mine], a.at[1, mine], side_peer)])

    first_send(og)

    window = pl.ds(pl.multiple_of(upper * (width // 2) + parity * 256, 128), 384)

    def expand(s):
        rows = pl.ds(s * tok, tok)
        value, slope = gelu_and_slope(dot_nn(nm[s], w_up[...]))
        hid[rows] = value.astype(BF16)
        prg[rows] = (slope * dot_nt(og[s], w_down[...])).astype(BF16)

    def turn(s):
        rows = pl.ds(s * tok, tok)
        ogt[:, rows] = og[s, :, window].T
        nmt[:, rows] = nm[s, :, window].T

    core_in = {(s, i): [] for s in (1, 2, 3) for i in range(2)}
    y_in, slot3 = {}, {}

    def across_core(s, i, rows):
        core_in[s, i].append(send(raw[i].at[s, rows], raw[i].at[s, rows], core_peer))

    def landed(s, i):
        (slot1[i][0] if s == 1 else slot2[i] if s == 2 else slot3[i]).wait_recv()
        if s == 2:
            slot3[i] = send(raw[i].at[2, mine], raw[i].at[3, mine], side_peer)
        if s != 1 or i not in direct:
            y_in[s, i] = send(raw[i].at[s, mine], raw[i].at[s, mine], y_peer)
        across_core(s, i, mine)

    def other_landed(s, i):
        (slot1[i][1] if s == 1 and i in direct else y_in[s, i]).wait_recv()
        across_core(s, i, theirs)

    def ready(s):
        take(core_in[s, 0] + core_in[s, 1])

    def take(copies):
        for one in copies:
            one.wait_recv()

    loads[2].wait()
    loads[3].wait()
    expand(0)
    part = dot_nt(prg[0:tok], w_up[...]).astype(BF16)
    for q in range(4):
        mp1[q % 2, q // 2] = part[q * share:(q + 1) * share]
    core1 = send(mp1.at[1 - c], ra1, core_peer)
    first_send(nm)

    for one in loads[4:]:
        one.wait()
    normed_in = norm_rows(inputs[...].astype(F32)).astype(BF16)
    values = dot_nt(normed_in, w_value_t[...]).astype(BF16)

    core1.wait_recv()
    sb1[...] = (mp1[c].astype(F32) + ra1[...].astype(F32)).astype(BF16)
    y1 = send(sb1, rb1, y_peer)

    column = lax.broadcasted_iota(jnp.int32, (tok, local), 1)

    def own_columns(array, h):
        keep = (column >= h * hdim) & (column < (h + 1) * hdim)
        return jnp.where(keep, array, jnp.zeros_like(array))

    total = dot_nn(maps[0], own_columns(values, 0))
    for h in range(1, heads_here):
        total = total + dot_nn(maps[h], own_columns(values, h))
    attd[...] = total.astype(BF16)
    att_x = send(attd, attd_p, x_peer)

    def halves(array, ref):
        turned = array.T
        for i in range(8):
            ref[i % 2, i // 2] = turned[i * piece:(i + 1) * piece]

    pair = pl.ds(c * 2, 2)
    halves(normed_in, nint)
    nint_x = send(nint.at[1 - x, pair], nint_p.at[pair], x_peer)
    turn(0)
    landed(2, 0)
    landed(1, 0)
    mid_core = []
    y1.wait_recv()
    for b in range(2):
        rows = quarter(b * 2 + c)
        grad = mp1[c, b].astype(F32) + ra1[b].astype(F32) + rb1[b].astype(F32)
        own = og[0, rows].astype(F32) + norm_back(middle[rows].astype(F32), grad)
        mid_rows[b] = own
        midb[rows] = own.astype(BF16)
        mid_core.append(send(midb.at[rows], midb.at[rows], core_peer))
    nint_x.wait_recv()
    nint_core = send(nint_p.at[pair], nint_p.at[pair], core_peer)
    take(mid_core)
    halves(midb[...], midbt)
    midbt_x = send(midbt.at[1 - x, pair], midbt_p.at[pair], x_peer)
    att_grad = dot_nt(midb[...], w_out[...]).astype(BF16)
    total = dot_tn(maps[0], own_columns(att_grad, 0))
    for h in range(1, heads_here):
        total = total + dot_tn(maps[h], own_columns(att_grad, h))
    vgr[...] = total.astype(BF16)
    vgr_x = send(vgr, vgr_p, x_peer)
    landed(2, 1)
    landed(1, 1)
    other_landed(2, 0)
    other_landed(1, 0)
    part = dot_nn(vgr[...], w_value_t[...]).astype(BF16)
    for q in range(4):
        mp2[q % 2, q // 2] = part[q * share:(q + 1) * share]
    core2 = send(mp2.at[1 - c], ra2, core_peer)

    def products(left, left_p, right, right_p, part_ref, send_ref):
        flat = 4 * piece
        total = dot_nn(left[x].reshape(flat, tok), right[...])
        total = total + dot_nn(left_p[...].reshape(flat, tok), right_p[...])
        for i in range(4):
            one = total[i * piece:(i + 1) * piece]
            part_ref[i % 2, i // 2] = one
            send_ref[i % 2, i // 2] = one.astype(BF16)

    midbt_x.wait_recv()
    midbt_core = send(midbt_p.at[pair], midbt_p.at[pair], core_peer)
    att_x.wait_recv()
    midbt_core.wait_recv()
    products(midbt, midbt_p, attd, attd_p, go_part, go_send)
    go_side = send(go_send.at[1 - parity], go_recv, side_peer)
    nint_core.wait_recv()
    vgr_x.wait_recv()
    products(nint, nint_p, vgr, vgr_p, gv_part, gv_send)
    gv_side = send(gv_send.at[1 - parity], gv_recv, side_peer)
    landed(3, 0)
    other_landed(2, 1)
    other_landed(1, 1)
    landed(3, 1)
    core2.wait_recv()
    sb2[...] = (mp2[c, 1 - y].astype(F32) + ra2[1 - y].astype(F32)).astype(BF16)
    y2 = send(sb2, rb2, y_peer)
    ready(1)
    expand(1)
    turn(1)
    ready(2)
    expand(2)
    turn(2)

    def halve(side, part_ref, recv, pass_ref, last):
        side.wait_recv()
        other = 1 - upper
        pass_ref[...] = (part_ref[parity, other] + recv[other].astype(F32)).astype(BF16)
        return send(pass_ref, last, cross_peer)

    other_landed(3, 0)
    go_cross = halve(go_side, go_part, go_recv, go_pass, go_last)
    span = 2 * piece
    rows = pl.ds(pl.multiple_of(parity * 64, 64), span)
    done = slice(0, 3 * tok)
    for i, (left, right) in enumerate(((ogt, hid), (nmt, prg))):
        mlp_part[:, i * ff:(i + 1) * ff] = dot_nn(left[rows, done], right[done])
    take(core_in[3, 0])
    grad_h[...] = dot_nt(og[3], w_down[...])
    ogt[:, 3 * tok:4 * tok] = og[3, :, window].T
    other_landed(3, 1)
    take(core_in[3, 1])
    last = slice(3 * tok, 4 * tok)
    mirror = []

    def finish(i, left, right):
        both = mlp_part[:, i * ff:(i + 1) * ff] + dot_nn(left[rows, last], right[last])
        mlp_part[:, i * ff:(i + 1) * ff] = both
        mlp_send[i, 0] = both[0:piece].astype(BF16)
        mlp_send[i, 1] = both[piece:span].astype(BF16)
        mirror.append(send(mlp_send.at[i, 1 - x], mlp_recv.at[i], x_peer))

    value, slope = gelu_and_slope(dot_nn(nm[3], w_up[...]))
    hid[last] = value.astype(BF16)
    finish(0, ogt, hid)
    gv_cross = halve(gv_side, gv_part, gv_recv, gv_pass, gv_last)
    prg[last] = (slope * grad_h[...]).astype(BF16)
    nmt[:, last] = nm[3, :, window].T
    finish(1, nmt, prg)
    y2.wait_recv()
    grad = mp2[c, y].astype(F32) + ra2[y].astype(F32) + rb2[...].astype(F32)
    in_grad[...] = (mid_rows[y] + norm_back(inputs[mine].astype(F32), grad)).astype(BF16)
    go_cross.wait_recv()
    go_sum[...] = go_part[parity, upper] + go_recv[upper].astype(F32) + go_last[...].astype(F32)
    gv_cross.wait_recv()
    gv_sum[...] = gv_part[parity, upper] + gv_recv[upper].astype(F32) + gv_last[...].astype(F32)
    own = pl.ds(pl.multiple_of(x * piece, piece), piece)
    for i, total in enumerate((down_sum, up_sum)):
        mirror[i].wait_recv()
        total[...] = mlp_part[own, i * ff:(i + 1) * ff] + mlp_recv[i].astype(F32)
    for one in started:
        one.wait_send()


def copy_kernel(*refs):
    sem = refs[-1]
    moves = [pltpu.make_async_copy(refs[i], refs[5 + i], sem.at[i]) for i in range(5)]
    for one in moves:
        one.start()
    for one in moves:
        one.wait()


def on_device_fused(inputs, middle, out_grad, cached_maps, w_value, w_out, w_up, w_down):
    tok, width = inputs.shape
    local, ff = w_value.shape[1], w_up.shape[1]
    heads_here = cached_maps.shape[1]
    piece = width // lax.axis_size("img")
    share = tok // 4
    vmem = pl.BlockSpec(memory_space=pltpu.VMEM)
    shape = jax.ShapeDtypeStruct
    results = (
        shape((share, width), BF16),
        shape((piece, local), F32),
        shape((piece, local), F32),
        shape((piece, ff), F32),
        shape((piece, ff), F32),
    )
    sums = pl.pallas_call(
        block_kernel,
        out_shape=results,
        in_specs=[pl.BlockSpec(memory_space=pl.ANY)] * 8,
        out_specs=(vmem,) * 5,
        scratch_shapes=[
            pltpu.VMEM((tok, width), BF16),
            pltpu.VMEM((tok, width), BF16),
            pltpu.VMEM((heads_here, tok, tok), BF16),
            pltpu.VMEM((local, width), BF16),
            pltpu.VMEM((local, width), BF16),
            pltpu.VMEM((width, ff), BF16),
            pltpu.VMEM((ff, width), BF16),
            pltpu.VMEM((4, tok, width), BF16),
            pltpu.VMEM((4, tok, width), BF16),
            pltpu.VMEM((384, 4 * tok), BF16),
            pltpu.VMEM((384, 4 * tok), BF16),
            pltpu.VMEM((4 * tok, ff), BF16),
            pltpu.VMEM((4 * tok, ff), BF16),
            pltpu.VMEM((tok, ff), F32),
            pltpu.VMEM((2 * piece, 2 * ff), F32),
            pltpu.VMEM((2, 2, piece, ff), BF16),
            pltpu.VMEM((2, piece, ff), BF16),
            pltpu.VMEM((2, 2, share, width), BF16),
            pltpu.VMEM((2, share, width), BF16),
            pltpu.VMEM((2, share, width), BF16),
            pltpu.VMEM((2, share, width), BF16),
            pltpu.VMEM((2, 2, share, width), BF16),
            pltpu.VMEM((2, share, width), BF16),
            pltpu.VMEM((share, width), BF16),
            pltpu.VMEM((share, width), BF16),
            pltpu.VMEM((2, share, width), F32),
            pltpu.VMEM((tok, width), BF16),
            pltpu.VMEM((2, 4, piece, tok), BF16),
            pltpu.VMEM((4, piece, tok), BF16),
            pltpu.VMEM((2, 4, piece, tok), BF16),
            pltpu.VMEM((4, piece, tok), BF16),
            pltpu.VMEM((tok, local), BF16),
            pltpu.VMEM((tok, local), BF16),
            pltpu.VMEM((tok, local), BF16),
            pltpu.VMEM((tok, local), BF16),
        ] + [
            pltpu.VMEM((2, 2, piece, local), F32),
            pltpu.VMEM((2, 2, piece, local), BF16),
            pltpu.VMEM((2, piece, local), BF16),
            pltpu.VMEM((piece, local), BF16),
            pltpu.VMEM((piece, local), BF16),
        ] * 2 + [
            pltpu.SemaphoreType.DMA((8,)),
            pltpu.SemaphoreType.DMA((COPIES,)),
            pltpu.SemaphoreType.DMA((COPIES,)),
        ],
        compiler_params=pltpu.CompilerParams(
            collective_id=0, has_side_effects=True, vmem_limit_bytes=56 * 1024 * 1024
        ),
    )(inputs, middle, out_grad, cached_maps[0], w_value.T, w_out, w_up, w_down)
    anywhere = pl.BlockSpec(memory_space=pl.ANY)
    in_grad, value_rows, out_rows_t, up_rows, down_rows_t = pl.pallas_call(
        copy_kernel,
        out_shape=results,
        in_specs=[vmem] * 5,
        out_specs=(anywhere,) * 5,
        scratch_shapes=[pltpu.SemaphoreType.DMA((5,))],
    )(*sums)
    return in_grad, value_rows, out_rows_t.T, up_rows, down_rows_t.T


def solution(mesh):
    fused = mesh.shape["img"] == 8 and mesh.shape["head"] == 4
    return jax.shard_map(
        on_device_fused if fused else on_device,
        mesh=mesh,
        in_specs=(
            P("img", None),
            P("img", None),
            P("img", None),
            P("img", "head", None, None),
            P(None, "head"),
            P("head", None),
            P(None, "head"),
            P("head", None),
        ),
        out_specs=(
            P(("img", "head"), None),
            P("img", "head"),
            P("head", "img"),
            P("img", "head"),
            P("head", "img"),
        ),
        check_vma=False,
    )
```

```python
import jax
import jax.numpy as jnp
from jax import lax
from jax.experimental import pallas as pl
from jax.experimental.pallas import tpu as pltpu
from jax.sharding import PartitionSpec as P


def norm_rows(rows):
    centre = rows - jnp.mean(rows, axis=-1, keepdims=True)
    spread = jnp.mean(centre * centre, axis=-1, keepdims=True)
    return centre * lax.rsqrt(spread + 1e-06)


def norm_back(rows, grad):
    centre = rows - jnp.mean(rows, axis=-1, keepdims=True)
    factor = lax.rsqrt(jnp.mean(centre * centre, axis=-1, keepdims=True) + 1e-06)
    normed = centre * factor
    return factor * (
        grad
        - jnp.mean(grad, axis=-1, keepdims=True)
        - normed * jnp.mean(grad * normed, axis=-1, keepdims=True)
    )


def gelu_tanh(pre):
    return jax.nn.gelu(pre, approximate=True)


def on_device(inputs, middle, out_grad, cached_maps, w_value, w_out, w_up, w_down):
    tok_rows = inputs.shape[0]
    heads_here = cached_maps.shape[1]
    share = tok_rows // lax.axis_size("head")
    first = lax.axis_index("head") * share
    maps_here = cached_maps[0]
    normed_in = norm_rows(inputs.astype(jnp.float32)).astype(jnp.bfloat16)
    values = jnp.dot(normed_in, w_value, preferred_element_type=jnp.float32).astype(jnp.bfloat16)
    head_size = values.shape[1] // heads_here
    attended = jnp.einsum(
        "htk,khd->thd",
        maps_here,
        values.reshape(tok_rows, heads_here, head_size),
        preferred_element_type=jnp.float32,
    )
    attended = attended.astype(jnp.bfloat16).reshape(tok_rows, -1)
    middle_f = middle.astype(jnp.float32)
    normed_mid = norm_rows(middle_f).astype(jnp.bfloat16)
    pre = jnp.dot(normed_mid, w_up, preferred_element_type=jnp.float32)
    hidden = gelu_tanh(pre).astype(jnp.bfloat16)
    hidden_grad = jnp.einsum("td,fd->tf", out_grad, w_down, preferred_element_type=jnp.float32)
    pre_grad = jax.vjp(gelu_tanh, pre)[1](hidden_grad)[0].astype(jnp.bfloat16)
    down_term = jnp.einsum("tf,td->fd", hidden, out_grad, preferred_element_type=jnp.float32)
    mid_part = jnp.einsum("tf,df->td", pre_grad, w_up, preferred_element_type=jnp.float32)
    out_rows = lax.dynamic_slice_in_dim(out_grad, first, share, 0).astype(jnp.float32)
    mid_share = lax.psum_scatter(mid_part, "head", scatter_dimension=0, tiled=True)
    mid_own = out_rows + norm_back(lax.dynamic_slice_in_dim(middle_f, first, share, 0), mid_share)
    mid_grad_b = lax.all_gather(mid_own.astype(jnp.bfloat16), "head", axis=0, tiled=True)
    outproj_term = jnp.einsum("te,td->ed", attended, mid_grad_b, preferred_element_type=jnp.float32)
    att_grad = jnp.einsum(
        "td,ed->te", mid_grad_b, w_out, preferred_element_type=jnp.float32
    ).astype(jnp.bfloat16)
    value_grad = jnp.einsum(
        "htk,thd->khd",
        maps_here,
        att_grad.reshape(tok_rows, heads_here, head_size),
        preferred_element_type=jnp.float32,
    )
    value_grad = value_grad.astype(jnp.bfloat16).reshape(tok_rows, -1)
    input_part = jnp.einsum("te,de->td", value_grad, w_value, preferred_element_type=jnp.float32)
    inputs_own = lax.dynamic_slice_in_dim(inputs, first, share, 0).astype(jnp.float32)
    input_share = lax.psum_scatter(input_part, "head", scatter_dimension=0, tiled=True)
    in_grad = (mid_own + norm_back(inputs_own, input_share)).astype(jnp.bfloat16)
    picked = normed_mid
    up_term = jnp.einsum("tr,tf->rf", picked, pre_grad, preferred_element_type=jnp.float32)
    picked = normed_in
    value_term = jnp.einsum("tr,te->re", picked, value_grad, preferred_element_type=jnp.float32)
    grad_down, grad_out = (
        lax.psum_scatter(down_term, "img", scatter_dimension=1, tiled=True),
        lax.psum_scatter(outproj_term, "img", scatter_dimension=1, tiled=True),
    )
    grad_up, grad_value = (
        lax.psum_scatter(up_term, "img", scatter_dimension=0, tiled=True),
        lax.psum_scatter(value_term, "img", scatter_dimension=0, tiled=True),
    )
    return (in_grad, grad_value, grad_out, grad_up, grad_down)


MESH = pl.DeviceIdType.MESH
F32 = jnp.float32
BF16 = jnp.bfloat16
COPIES = 64
GELU_C = 0.7978845608028654


def dot_nn(a, b):
    return lax.dot_general(a, b, (((1,), (0,)), ((), ())), preferred_element_type=F32)


def dot_nt(a, b):
    return lax.dot_general(a, b, (((1,), (1,)), ((), ())), preferred_element_type=F32)


def dot_tn(a, b):
    return lax.dot_general(a, b, (((0,), (0,)), ((), ())), preferred_element_type=F32)


def gelu_and_slope(pre):
    square = pre * pre
    tanh = jnp.tanh(GELU_C * pre * (1.0 + 0.044715 * square))
    half = 0.5 * (1.0 + tanh)
    slope = half + 0.5 * pre * (1.0 - tanh * tanh) * (GELU_C * (1.0 + 3 * 0.044715 * square))
    return pre * half, slope


def block_kernel(
    inputs_h, middle_h, out_grad_h, maps_h, w_value_h, w_out_h, w_up_h, w_down_h,
    in_grad_h, gv_sum_h, go_sum_h, mlp_own_h, mlp_recv,
    inputs, middle, maps, w_value_t, w_out, w_up, w_down,
    og, nm, og_cut, ogt, nmt, hid, prg, grad_h, in_grad, gv_sum, go_sum, mlp_part, mlp_send,
    mp1, ra1, sb1, rb1, mp2, ra2, sb2, rb2, mid_rows, midb,
    nint, nint_p, midbt, midbt_p, attd, attd_p, vgr, vgr_p,
    go_part, go_send, go_recv, go_pass, go_last, gv_part, gv_send, gv_recv, gv_pass, gv_last,
    local_sem, send_sem, recv_sem,
):
    tok, width = inputs.shape
    share = tok // 4
    heads_here = maps.shape[0]
    local = attd.shape[1]
    hdim = local // heads_here
    ff = w_up.shape[1]
    piece = mlp_send.shape[2]
    img = lax.axis_index("img")
    head = lax.axis_index("head")
    z, x = img // 2, img % 2
    y, c = head // 2, head % 2
    upper, parity = z // 2, z % 2
    x_peer = {"img": z * 2 + (1 - x)}
    side_peer = {"img": (upper * 2 + 1 - parity) * 2 + x}
    cross_peer = {"img": ((1 - upper) * 2 + parity) * 2 + x}
    y_peer = {"head": (1 - y) * 2 + c}
    core_peer = {"head": y * 2 + (1 - c)}
    used = []

    def copy(src, dst, peer):
        sem = len(used)
        used.append(sem)
        return pltpu.make_async_remote_copy(
            src_ref=src, dst_ref=dst, send_sem=send_sem.at[sem], recv_sem=recv_sem.at[sem],
            device_id=peer, device_id_type=MESH,
        )

    started = []

    def send(src, dst, peer):
        one = copy(src, dst, peer)
        one.start()
        started.append(one)
        return one

    def quarter(h):
        return pl.ds(pl.multiple_of(h * share, share), share)

    mine, theirs = quarter(head), quarter((1 - y) * 2 + c)

    barrier = pltpu.get_barrier_semaphore()
    for peer in (x_peer, side_peer, cross_peer, y_peer, core_peer):
        pl.semaphore_signal(barrier, inc=1, device_id=peer, device_id_type=MESH)
    loads = [
        pltpu.make_async_copy(src, dst, local_sem.at[i])
        for i, (src, dst) in enumerate([
            (middle_h, middle), (out_grad_h, og.at[0]), (w_up_h, w_up), (w_down_h, w_down),
            (inputs_h, inputs), (w_value_h, w_value_t), (maps_h, maps), (w_out_h, w_out),
        ])
    ]
    for one in loads[:4]:
        one.start()
    loads[0].wait()
    for one in loads[4:]:
        one.start()
    nm[0] = norm_rows(middle[...].astype(F32)).astype(BF16)
    loads[1].wait()
    pl.semaphore_wait(barrier, 5)
    raw = (nm, og)
    direct = ()
    slot1, slot2 = [], []

    def first_send(a):
        slot2.append(send(a.at[0, mine], a.at[2, mine], cross_peer))
        slot1.append([send(a.at[0, mine], a.at[1, mine], side_peer)])

    first_send(nm)

    window = pl.ds(pl.multiple_of(upper * (width // 2) + parity * 256, 128), 384)

    def expand(s):
        rows = pl.ds(s * tok, tok)
        value, slope = gelu_and_slope(dot_nn(nm[s], w_up[...]))
        hid[rows] = value.astype(BF16)
        prg[rows] = (slope * dot_nt(og[s], w_down[...])).astype(BF16)

    def turn(s):
        rows = pl.ds(s * tok, tok)
        ogt[:, rows] = og[s, :, window].T
        nmt[:, rows] = nm[s, :, window].T

    core_in = {(s, i): [] for s in (1, 2, 3) for i in range(2)}
    y_in, slot3, cut = {}, {}, {}
    side_window = pl.ds(pl.multiple_of(upper * (width // 2) + (1 - parity) * 256, 128), 384)

    def across_core(s, i, rows):
        core_in[s, i].append(send(raw[i].at[s, rows], raw[i].at[s, rows], core_peer))

    def landed(s, i):
        (slot1[i][0] if s == 1 else slot2[i] if s == 2 else slot3[i]).wait_recv()
        if s == 2 and i == 1:
            cut["first"] = send(og.at[2, mine, side_window], og_cut.at[mine], side_peer)
        if s == 2:
            slot3[i] = send(raw[i].at[2, mine], raw[i].at[3, mine], side_peer)
        if s != 1 or i not in direct:
            y_in[s, i] = send(raw[i].at[s, mine], raw[i].at[s, mine], y_peer)
        across_core(s, i, mine)

    def other_landed(s, i):
        (slot1[i][1] if s == 1 and i in direct else y_in[s, i]).wait_recv()
        across_core(s, i, theirs)

    def cut_landed():
        cut["first"].wait_recv()
        cut["y"] = send(og_cut.at[mine], og_cut.at[mine], y_peer)
        cut["core"] = [send(og_cut.at[mine], og_cut.at[mine], core_peer)]

    def other_cut_landed():
        cut["y"].wait_recv()
        cut["core"].append(send(og_cut.at[theirs], og_cut.at[theirs], core_peer))

    def ready(s):
        take(core_in[s, 0] + core_in[s, 1])

    def take(copies):
        for one in copies:
            one.wait_recv()

    loads[2].wait()
    loads[3].wait()
    expand(0)
    part = dot_nt(prg[0:tok], w_up[...]).astype(BF16)
    for q in range(4):
        mp1[q % 2, q // 2] = part[q * share:(q + 1) * share]
    core1 = send(mp1.at[1 - c], ra1, core_peer)
    first_send(og)

    for one in loads[4:]:
        one.wait()
    normed_in = norm_rows(inputs[...].astype(F32)).astype(BF16)
    values = dot_nt(normed_in, w_value_t[...]).astype(BF16)

    core1.wait_recv()
    sb1[...] = (mp1[c].astype(F32) + ra1[...].astype(F32)).astype(BF16)
    y1 = send(sb1, rb1, y_peer)

    column = lax.broadcasted_iota(jnp.int32, (tok, local), 1)

    def own_columns(array, h):
        keep = (column >= h * hdim) & (column < (h + 1) * hdim)
        return jnp.where(keep, array, jnp.zeros_like(array))

    total = dot_nn(maps[0], own_columns(values, 0))
    for h in range(1, heads_here):
        total = total + dot_nn(maps[h], own_columns(values, h))
    attd[...] = total.astype(BF16)
    att_x = send(attd, attd_p, x_peer)

    def halves(array, ref):
        turned = array.T
        for i in range(8):
            ref[i % 2, i // 2] = turned[i * piece:(i + 1) * piece]

    pair = pl.ds(c * 2, 2)
    halves(normed_in, nint)
    nint_x = send(nint.at[1 - x, pair], nint_p.at[pair], x_peer)
    turn(0)
    landed(2, 0)
    landed(1, 0)
    mid_core = []
    y1.wait_recv()
    for b in range(2):
        rows = quarter(b * 2 + c)
        grad = mp1[c, b].astype(F32) + ra1[b].astype(F32) + rb1[b].astype(F32)
        own = og[0, rows].astype(F32) + norm_back(middle[rows].astype(F32), grad)
        mid_rows[b] = own
        midb[rows] = own.astype(BF16)
        mid_core.append(send(midb.at[rows], midb.at[rows], core_peer))
    nint_x.wait_recv()
    nint_core = send(nint_p.at[pair], nint_p.at[pair], core_peer)
    take(mid_core)
    halves(midb[...], midbt)
    midbt_x = send(midbt.at[1 - x, pair], midbt_p.at[pair], x_peer)
    att_grad = dot_nt(midb[...], w_out[...]).astype(BF16)
    total = dot_tn(maps[0], own_columns(att_grad, 0))
    for h in range(1, heads_here):
        total = total + dot_tn(maps[h], own_columns(att_grad, h))
    vgr[...] = total.astype(BF16)
    vgr_x = send(vgr, vgr_p, x_peer)
    landed(2, 1)
    landed(1, 1)
    other_landed(2, 0)
    other_landed(1, 0)
    part = dot_nn(vgr[...], w_value_t[...]).astype(BF16)
    for q in range(4):
        mp2[q % 2, q // 2] = part[q * share:(q + 1) * share]
    core2 = send(mp2.at[1 - c], ra2, core_peer)

    def products(left, left_p, right, right_p, part_ref, send_ref):
        flat = 4 * piece
        total = dot_nn(left[x].reshape(flat, tok), right[...])
        total = total + dot_nn(left_p[...].reshape(flat, tok), right_p[...])
        for i in range(4):
            one = total[i * piece:(i + 1) * piece]
            part_ref[i % 2, i // 2] = one
            send_ref[i % 2, i // 2] = one.astype(BF16)

    midbt_x.wait_recv()
    midbt_core = send(midbt_p.at[pair], midbt_p.at[pair], core_peer)
    att_x.wait_recv()
    midbt_core.wait_recv()
    products(midbt, midbt_p, attd, attd_p, go_part, go_send)
    go_side = send(go_send.at[1 - parity], go_recv, side_peer)
    nint_core.wait_recv()
    vgr_x.wait_recv()
    products(nint, nint_p, vgr, vgr_p, gv_part, gv_send)
    gv_side = send(gv_send.at[1 - parity], gv_recv, side_peer)
    landed(3, 0)
    other_landed(2, 1)
    other_landed(1, 1)
    cut_landed()
    landed(3, 1)
    core2.wait_recv()
    sb2[...] = (mp2[c, 1 - y].astype(F32) + ra2[1 - y].astype(F32)).astype(BF16)
    y2 = send(sb2, rb2, y_peer)
    ready(1)
    expand(1)
    turn(1)
    ready(2)
    expand(2)
    turn(2)

    def halve(side, part_ref, recv, pass_ref, last):
        side.wait_recv()
        other = 1 - upper
        pass_ref[...] = (part_ref[parity, other] + recv[other].astype(F32)).astype(BF16)
        return send(pass_ref, last, cross_peer)

    other_landed(3, 0)
    go_cross = halve(go_side, go_part, go_recv, go_pass, go_last)
    span = 2 * piece
    rows = pl.ds(pl.multiple_of(parity * 64, 64), span)
    done = slice(0, 3 * tok)
    for i, (left, right) in enumerate(((ogt, hid), (nmt, prg))):
        mlp_part[:, i * ff:(i + 1) * ff] = dot_nn(left[rows, done], right[done])
    other_cut_landed()
    last = slice(3 * tok, 4 * tok)
    mirror = []

    def finish(i, left, right):
        both = mlp_part[:, i * ff:(i + 1) * ff] + dot_nn(left[rows, last], right[last])
        mlp_part[:, i * ff:(i + 1) * ff] = both
        mlp_send[i, 0] = both[0:piece].astype(BF16)
        mlp_send[i, 1] = both[piece:span].astype(BF16)
        mirror.append(send(mlp_send.at[i, 1 - x], mlp_recv.at[i], x_peer))

    take(core_in[3, 0])
    value, slope = gelu_and_slope(dot_nn(nm[3], w_up[...]))
    hid[last] = value.astype(BF16)
    grad_h[...] = slope
    take(cut["core"])
    ogt[:, last] = og_cut[...].T
    finish(0, ogt, hid)
    nmt[:, last] = nm[3, :, window].T
    other_landed(3, 1)
    gv_cross = halve(gv_side, gv_part, gv_recv, gv_pass, gv_last)
    take(core_in[3, 1])
    prg[last] = (grad_h[...] * dot_nt(og[3], w_down[...])).astype(BF16)
    finish(1, nmt, prg)
    y2.wait_recv()
    grad = mp2[c, y].astype(F32) + ra2[y].astype(F32) + rb2[...].astype(F32)
    in_grad[...] = (mid_rows[y] + norm_back(inputs[mine].astype(F32), grad)).astype(BF16)
    stores = []

    def store(src, dst):
        one = pltpu.make_async_copy(src, dst, local_sem.at[8 + len(stores)])
        one.start()
        stores.append(one)

    own = pl.ds(pl.multiple_of(x * piece, piece), piece)
    store(in_grad, in_grad_h)
    for i in range(2):
        store(mlp_part.at[own, pl.ds(i * ff, ff)], mlp_own_h.at[i])
    go_cross.wait_recv()
    go_sum[...] = go_part[parity, upper] + go_recv[upper].astype(F32) + go_last[...].astype(F32)
    store(go_sum, go_sum_h)
    gv_cross.wait_recv()
    gv_sum[...] = gv_part[parity, upper] + gv_recv[upper].astype(F32) + gv_last[...].astype(F32)
    store(gv_sum, gv_sum_h)
    for one in stores:
        one.wait()
    for one in mirror:
        one.wait_recv()
    for one in started:
        one.wait_send()


def last_sums_kernel(
    in_grad, gv_sum, go_sum, mlp_own, mlp_recv, in_grad_h, gv_sum_h, go_sum_h, up_sum_h, down_sum_h, sums, sem
):
    stores = []

    def store(src, dst):
        one = pltpu.make_async_copy(src, dst, sem.at[len(stores)])
        one.start()
        stores.append(one)

    for i, dst in enumerate((down_sum_h, up_sum_h)):
        sums[i] = mlp_own[i] + mlp_recv[i].astype(F32)
        store(sums.at[i], dst)
    store(in_grad, in_grad_h)
    store(gv_sum, gv_sum_h)
    store(go_sum, go_sum_h)
    for one in stores:
        one.wait()


def on_device_fused(inputs, middle, out_grad, cached_maps, w_value, w_out, w_up, w_down):
    tok, width = inputs.shape
    local, ff = w_value.shape[1], w_up.shape[1]
    heads_here = cached_maps.shape[1]
    piece = width // lax.axis_size("img")
    share = tok // 4
    vmem = pl.BlockSpec(memory_space=pltpu.VMEM)
    anywhere = pl.BlockSpec(memory_space=pl.ANY)
    shape = jax.ShapeDtypeStruct
    results = (
        shape((share, width), BF16),
        shape((piece, local), F32),
        shape((piece, local), F32),
        shape((piece, ff), F32),
        shape((piece, ff), F32),
    )
    sums = pl.pallas_call(
        block_kernel,
        out_shape=results[:3] + (shape((2, piece, ff), F32), shape((2, piece, ff), BF16)),
        in_specs=[anywhere] * 8,
        out_specs=(anywhere,) * 5,
        scratch_shapes=[
            pltpu.VMEM((tok, width), BF16),
            pltpu.VMEM((tok, width), BF16),
            pltpu.VMEM((heads_here, tok, tok), BF16),
            pltpu.VMEM((local, width), BF16),
            pltpu.VMEM((local, width), BF16),
            pltpu.VMEM((width, ff), BF16),
            pltpu.VMEM((ff, width), BF16),
            pltpu.VMEM((4, tok, width), BF16),
            pltpu.VMEM((4, tok, width), BF16),
            pltpu.VMEM((tok, 384), BF16),
            pltpu.VMEM((384, 4 * tok), BF16),
            pltpu.VMEM((384, 4 * tok), BF16),
            pltpu.VMEM((4 * tok, ff), BF16),
            pltpu.VMEM((4 * tok, ff), BF16),
            pltpu.VMEM((tok, ff), F32),
            pltpu.VMEM((share, width), BF16),
            pltpu.VMEM((piece, local), F32),
            pltpu.VMEM((piece, local), F32),
            pltpu.VMEM((2 * piece, 2 * ff), F32),
            pltpu.VMEM((2, 2, piece, ff), BF16),
            pltpu.VMEM((2, 2, share, width), BF16),
            pltpu.VMEM((2, share, width), BF16),
            pltpu.VMEM((2, share, width), BF16),
            pltpu.VMEM((2, share, width), BF16),
            pltpu.VMEM((2, 2, share, width), BF16),
            pltpu.VMEM((2, share, width), BF16),
            pltpu.VMEM((share, width), BF16),
            pltpu.VMEM((share, width), BF16),
            pltpu.VMEM((2, share, width), F32),
            pltpu.VMEM((tok, width), BF16),
            pltpu.VMEM((2, 4, piece, tok), BF16),
            pltpu.VMEM((4, piece, tok), BF16),
            pltpu.VMEM((2, 4, piece, tok), BF16),
            pltpu.VMEM((4, piece, tok), BF16),
            pltpu.VMEM((tok, local), BF16),
            pltpu.VMEM((tok, local), BF16),
            pltpu.VMEM((tok, local), BF16),
            pltpu.VMEM((tok, local), BF16),
        ] + [
            pltpu.VMEM((2, 2, piece, local), F32),
            pltpu.VMEM((2, 2, piece, local), BF16),
            pltpu.VMEM((2, piece, local), BF16),
            pltpu.VMEM((piece, local), BF16),
            pltpu.VMEM((piece, local), BF16),
        ] * 2 + [
            pltpu.SemaphoreType.DMA((13,)),
            pltpu.SemaphoreType.DMA((COPIES,)),
            pltpu.SemaphoreType.DMA((COPIES,)),
        ],
        compiler_params=pltpu.CompilerParams(
            collective_id=0, has_side_effects=True, vmem_limit_bytes=56 * 1024 * 1024
        ),
    )(inputs, middle, out_grad, cached_maps[0], w_value.T, w_out, w_up, w_down)
    in_grad, value_rows, out_rows_t, up_rows, down_rows_t = pl.pallas_call(
        last_sums_kernel,
        out_shape=results,
        in_specs=[vmem] * 5,
        out_specs=(anywhere,) * 5,
        scratch_shapes=[pltpu.VMEM((2, piece, ff), F32), pltpu.SemaphoreType.DMA((5,))],
    )(*sums)
    return in_grad, value_rows, out_rows_t.T, up_rows, down_rows_t.T


def solution(mesh):
    fused = mesh.shape["img"] == 8 and mesh.shape["head"] == 4
    return jax.shard_map(
        on_device_fused if fused else on_device,
        mesh=mesh,
        in_specs=(
            P("img", None),
            P("img", None),
            P("img", None),
            P("img", "head", None, None),
            P(None, "head"),
            P("head", None),
            P(None, "head"),
            P("head", None),
        ),
        out_specs=(
            P(("img", "head"), None),
            P("img", "head"),
            P("head", "img"),
            P("img", "head"),
            P("head", "img"),
        ),
        check_vma=False,
    )
```

```python
import jax
import jax.numpy as jnp
from jax import lax
from jax.experimental import pallas as pl
from jax.experimental.pallas import tpu as pltpu
from jax.sharding import PartitionSpec as P


def norm_rows(rows):
    centre = rows - jnp.mean(rows, axis=-1, keepdims=True)
    spread = jnp.mean(centre * centre, axis=-1, keepdims=True)
    return centre * lax.rsqrt(spread + 1e-06)


def norm_back(rows, grad):
    centre = rows - jnp.mean(rows, axis=-1, keepdims=True)
    factor = lax.rsqrt(jnp.mean(centre * centre, axis=-1, keepdims=True) + 1e-06)
    normed = centre * factor
    return factor * (
        grad
        - jnp.mean(grad, axis=-1, keepdims=True)
        - normed * jnp.mean(grad * normed, axis=-1, keepdims=True)
    )


def gelu_tanh(pre):
    return jax.nn.gelu(pre, approximate=True)


def on_device(inputs, middle, out_grad, cached_maps, w_value, w_out, w_up, w_down):
    tok_rows = inputs.shape[0]
    heads_here = cached_maps.shape[1]
    share = tok_rows // lax.axis_size("head")
    first = lax.axis_index("head") * share
    maps_here = cached_maps[0]
    normed_in = norm_rows(inputs.astype(jnp.float32)).astype(jnp.bfloat16)
    values = jnp.dot(normed_in, w_value, preferred_element_type=jnp.float32).astype(jnp.bfloat16)
    head_size = values.shape[1] // heads_here
    attended = jnp.einsum(
        "htk,khd->thd",
        maps_here,
        values.reshape(tok_rows, heads_here, head_size),
        preferred_element_type=jnp.float32,
    )
    attended = attended.astype(jnp.bfloat16).reshape(tok_rows, -1)
    middle_f = middle.astype(jnp.float32)
    normed_mid = norm_rows(middle_f).astype(jnp.bfloat16)
    pre = jnp.dot(normed_mid, w_up, preferred_element_type=jnp.float32)
    hidden = gelu_tanh(pre).astype(jnp.bfloat16)
    hidden_grad = jnp.einsum("td,fd->tf", out_grad, w_down, preferred_element_type=jnp.float32)
    pre_grad = jax.vjp(gelu_tanh, pre)[1](hidden_grad)[0].astype(jnp.bfloat16)
    down_term = jnp.einsum("tf,td->fd", hidden, out_grad, preferred_element_type=jnp.float32)
    mid_part = jnp.einsum("tf,df->td", pre_grad, w_up, preferred_element_type=jnp.float32)
    out_rows = lax.dynamic_slice_in_dim(out_grad, first, share, 0).astype(jnp.float32)
    mid_share = lax.psum_scatter(mid_part, "head", scatter_dimension=0, tiled=True)
    mid_own = out_rows + norm_back(lax.dynamic_slice_in_dim(middle_f, first, share, 0), mid_share)
    mid_grad_b = lax.all_gather(mid_own.astype(jnp.bfloat16), "head", axis=0, tiled=True)
    outproj_term = jnp.einsum("te,td->ed", attended, mid_grad_b, preferred_element_type=jnp.float32)
    att_grad = jnp.einsum(
        "td,ed->te", mid_grad_b, w_out, preferred_element_type=jnp.float32
    ).astype(jnp.bfloat16)
    value_grad = jnp.einsum(
        "htk,thd->khd",
        maps_here,
        att_grad.reshape(tok_rows, heads_here, head_size),
        preferred_element_type=jnp.float32,
    )
    value_grad = value_grad.astype(jnp.bfloat16).reshape(tok_rows, -1)
    input_part = jnp.einsum("te,de->td", value_grad, w_value, preferred_element_type=jnp.float32)
    inputs_own = lax.dynamic_slice_in_dim(inputs, first, share, 0).astype(jnp.float32)
    input_share = lax.psum_scatter(input_part, "head", scatter_dimension=0, tiled=True)
    in_grad = (mid_own + norm_back(inputs_own, input_share)).astype(jnp.bfloat16)
    picked = normed_mid
    up_term = jnp.einsum("tr,tf->rf", picked, pre_grad, preferred_element_type=jnp.float32)
    picked = normed_in
    value_term = jnp.einsum("tr,te->re", picked, value_grad, preferred_element_type=jnp.float32)
    grad_down, grad_out = (
        lax.psum_scatter(down_term, "img", scatter_dimension=1, tiled=True),
        lax.psum_scatter(outproj_term, "img", scatter_dimension=1, tiled=True),
    )
    grad_up, grad_value = (
        lax.psum_scatter(up_term, "img", scatter_dimension=0, tiled=True),
        lax.psum_scatter(value_term, "img", scatter_dimension=0, tiled=True),
    )
    return (in_grad, grad_value, grad_out, grad_up, grad_down)


MESH = pl.DeviceIdType.MESH
F32 = jnp.float32
BF16 = jnp.bfloat16
COPIES = 64
GELU_C = 0.7978845608028654


def dot_nn(a, b):
    return lax.dot_general(a, b, (((1,), (0,)), ((), ())), preferred_element_type=F32)


def dot_nt(a, b):
    return lax.dot_general(a, b, (((1,), (1,)), ((), ())), preferred_element_type=F32)


def dot_tn(a, b):
    return lax.dot_general(a, b, (((0,), (0,)), ((), ())), preferred_element_type=F32)


def gelu_and_slope(pre):
    square = pre * pre
    tanh = jnp.tanh(GELU_C * pre * (1.0 + 0.044715 * square))
    half = 0.5 * (1.0 + tanh)
    slope = half + 0.5 * pre * (1.0 - tanh * tanh) * (GELU_C * (1.0 + 3 * 0.044715 * square))
    return pre * half, slope


def block_kernel(
    inputs_h, middle_h, out_grad_h, maps_h, w_value_h, w_out_h, w_up_h, w_down_h,
    in_grad_h, gv_sum_h, go_sum_h, mlp_own_h, mlp_recv,
    inputs, middle, maps, w_value_t, w_out, w_up, w_down,
    og, nm, og_cut, ogt, nmt, hid, prg, grad_h, in_grad, gv_sum, go_sum, mlp_part, mlp_send,
    mp1, ra1, sb1, rb1, mp2, ra2, sb2, rb2, mid_rows, midb,
    nint, nint_p, midbt, midbt_p, attd, attd_p, vgr, vgr_p,
    go_part, go_send, go_recv, go_pass, go_last, gv_part, gv_send, gv_recv, gv_pass, gv_last,
    local_sem, send_sem, recv_sem,
):
    tok, width = inputs.shape
    share = tok // 4
    heads_here = maps.shape[0]
    local = attd.shape[1]
    hdim = local // heads_here
    ff = w_up.shape[1]
    piece = mlp_send.shape[2]
    img = lax.axis_index("img")
    head = lax.axis_index("head")
    z, x = img // 2, img % 2
    y, c = head // 2, head % 2
    upper, parity = z // 2, z % 2
    x_peer = {"img": z * 2 + (1 - x)}
    side_peer = {"img": (upper * 2 + 1 - parity) * 2 + x}
    cross_peer = {"img": ((1 - upper) * 2 + parity) * 2 + x}
    y_peer = {"head": (1 - y) * 2 + c}
    core_peer = {"head": y * 2 + (1 - c)}
    used = []

    def copy(src, dst, peer):
        sem = len(used)
        used.append(sem)
        return pltpu.make_async_remote_copy(
            src_ref=src, dst_ref=dst, send_sem=send_sem.at[sem], recv_sem=recv_sem.at[sem],
            device_id=peer, device_id_type=MESH,
        )

    started = []

    def send(src, dst, peer):
        one = copy(src, dst, peer)
        one.start()
        started.append(one)
        return one

    def quarter(h):
        return pl.ds(pl.multiple_of(h * share, share), share)

    mine, theirs = quarter(head), quarter((1 - y) * 2 + c)

    barrier = pltpu.get_barrier_semaphore()
    for peer in (x_peer, side_peer, cross_peer, y_peer, core_peer):
        pl.semaphore_signal(barrier, inc=1, device_id=peer, device_id_type=MESH)
    loads = [
        pltpu.make_async_copy(src, dst, local_sem.at[i])
        for i, (src, dst) in enumerate([
            (middle_h, middle), (out_grad_h, og.at[0]), (w_up_h, w_up), (w_down_h, w_down),
            (inputs_h, inputs), (w_value_h, w_value_t), (maps_h, maps), (w_out_h, w_out),
        ])
    ]
    for one in loads[:4]:
        one.start()
    loads[0].wait()
    for one in loads[4:]:
        one.start()
    nm[0] = norm_rows(middle[...].astype(F32)).astype(BF16)
    loads[1].wait()
    pl.semaphore_wait(barrier, 5)
    raw = (nm, og)
    direct = ()
    slot1, slot2 = [], []

    def first_send(a):
        slot2.append(send(a.at[0, mine], a.at[2, mine], cross_peer))
        slot1.append([send(a.at[0, mine], a.at[1, mine], side_peer)])

    first_send(nm)
    first_send(og)

    window = pl.ds(pl.multiple_of(upper * (width // 2) + parity * 256, 128), 384)

    def expand(s):
        rows = pl.ds(s * tok, tok)
        value, slope = gelu_and_slope(dot_nn(nm[s], w_up[...]))
        hid[rows] = value.astype(BF16)
        prg[rows] = (slope * dot_nt(og[s], w_down[...])).astype(BF16)

    def turn(s):
        rows = pl.ds(s * tok, tok)
        ogt[:, rows] = og[s, :, window].T
        nmt[:, rows] = nm[s, :, window].T

    core_in = {(s, i): [] for s in (1, 2, 3) for i in range(2)}
    y_in, slot3, cut = {}, {}, {}
    side_window = pl.ds(pl.multiple_of(upper * (width // 2) + (1 - parity) * 256, 128), 384)

    def across_core(s, i, rows):
        core_in[s, i].append(send(raw[i].at[s, rows], raw[i].at[s, rows], core_peer))

    def landed(s, i):
        (slot1[i][0] if s == 1 else slot2[i] if s == 2 else slot3[i]).wait_recv()
        if s == 2 and i == 1:
            cut["first"] = send(og.at[2, mine, side_window], og_cut.at[mine], side_peer)
        if s == 2:
            slot3[i] = send(raw[i].at[2, mine], raw[i].at[3, mine], side_peer)
        if s != 1 or i not in direct:
            y_in[s, i] = send(raw[i].at[s, mine], raw[i].at[s, mine], y_peer)
        across_core(s, i, mine)

    def other_landed(s, i):
        (slot1[i][1] if s == 1 and i in direct else y_in[s, i]).wait_recv()
        across_core(s, i, theirs)

    def cut_landed():
        cut["first"].wait_recv()
        cut["y"] = send(og_cut.at[mine], og_cut.at[mine], y_peer)
        cut["core"] = [send(og_cut.at[mine], og_cut.at[mine], core_peer)]

    def other_cut_landed():
        cut["y"].wait_recv()
        cut["core"].append(send(og_cut.at[theirs], og_cut.at[theirs], core_peer))

    def ready(s):
        take(core_in[s, 0] + core_in[s, 1])

    def take(copies):
        for one in copies:
            one.wait_recv()

    loads[2].wait()
    loads[3].wait()
    expand(0)
    part = dot_nt(prg[0:tok], w_up[...]).astype(BF16)
    for q in range(4):
        mp1[q % 2, q // 2] = part[q * share:(q + 1) * share]
    core1 = send(mp1.at[1 - c], ra1, core_peer)

    for one in loads[4:]:
        one.wait()
    normed_in = norm_rows(inputs[...].astype(F32)).astype(BF16)
    values = dot_nt(normed_in, w_value_t[...]).astype(BF16)

    core1.wait_recv()
    sb1[...] = (mp1[c].astype(F32) + ra1[...].astype(F32)).astype(BF16)
    y1 = send(sb1, rb1, y_peer)

    column = lax.broadcasted_iota(jnp.int32, (tok, local), 1)

    def own_columns(array, h):
        keep = (column >= h * hdim) & (column < (h + 1) * hdim)
        return jnp.where(keep, array, jnp.zeros_like(array))

    total = dot_nn(maps[0], own_columns(values, 0))
    for h in range(1, heads_here):
        total = total + dot_nn(maps[h], own_columns(values, h))
    attd[...] = total.astype(BF16)
    att_x = send(attd, attd_p, x_peer)

    def halves(array, ref):
        turned = array.T
        for i in range(8):
            ref[i % 2, i // 2] = turned[i * piece:(i + 1) * piece]

    pair = pl.ds(c * 2, 2)
    halves(normed_in, nint)
    nint_x = send(nint.at[1 - x, pair], nint_p.at[pair], x_peer)
    turn(0)
    landed(2, 0)
    landed(1, 0)
    mid_core = []
    y1.wait_recv()
    for b in range(2):
        rows = quarter(b * 2 + c)
        grad = mp1[c, b].astype(F32) + ra1[b].astype(F32) + rb1[b].astype(F32)
        own = og[0, rows].astype(F32) + norm_back(middle[rows].astype(F32), grad)
        mid_rows[b] = own
        midb[rows] = own.astype(BF16)
        mid_core.append(send(midb.at[rows], midb.at[rows], core_peer))
    nint_x.wait_recv()
    nint_core = send(nint_p.at[pair], nint_p.at[pair], core_peer)
    take(mid_core)
    halves(midb[...], midbt)
    midbt_x = send(midbt.at[1 - x, pair], midbt_p.at[pair], x_peer)
    att_grad = dot_nt(midb[...], w_out[...]).astype(BF16)
    total = dot_tn(maps[0], own_columns(att_grad, 0))
    for h in range(1, heads_here):
        total = total + dot_tn(maps[h], own_columns(att_grad, h))
    vgr[...] = total.astype(BF16)
    vgr_x = send(vgr, vgr_p, x_peer)
    landed(2, 1)
    landed(1, 1)
    other_landed(2, 0)
    other_landed(1, 0)
    part = dot_nn(vgr[...], w_value_t[...]).astype(BF16)
    for q in range(4):
        mp2[q % 2, q // 2] = part[q * share:(q + 1) * share]
    core2 = send(mp2.at[1 - c], ra2, core_peer)

    def products(left, left_p, right, right_p, part_ref, send_ref):
        flat = 4 * piece
        total = dot_nn(left[x].reshape(flat, tok), right[...])
        total = total + dot_nn(left_p[...].reshape(flat, tok), right_p[...])
        for i in range(4):
            one = total[i * piece:(i + 1) * piece]
            part_ref[i % 2, i // 2] = one
            send_ref[i % 2, i // 2] = one.astype(BF16)

    midbt_x.wait_recv()
    midbt_core = send(midbt_p.at[pair], midbt_p.at[pair], core_peer)
    att_x.wait_recv()
    midbt_core.wait_recv()
    products(midbt, midbt_p, attd, attd_p, go_part, go_send)
    go_side = send(go_send.at[1 - parity], go_recv, side_peer)
    nint_core.wait_recv()
    vgr_x.wait_recv()
    products(nint, nint_p, vgr, vgr_p, gv_part, gv_send)
    gv_side = send(gv_send.at[1 - parity], gv_recv, side_peer)
    landed(3, 0)
    other_landed(2, 1)
    other_landed(1, 1)
    cut_landed()
    landed(3, 1)
    ready(1)
    expand(1)
    turn(1)
    ready(2)
    expand(2)
    turn(2)

    def halve(side, part_ref, recv, pass_ref, last):
        side.wait_recv()
        other = 1 - upper
        pass_ref[...] = (part_ref[parity, other] + recv[other].astype(F32)).astype(BF16)
        return send(pass_ref, last, cross_peer)

    other_landed(3, 0)
    go_cross = halve(go_side, go_part, go_recv, go_pass, go_last)
    span = 2 * piece
    rows = pl.ds(pl.multiple_of(parity * 64, 64), span)
    done = slice(0, 3 * tok)
    for i, (left, right) in enumerate(((ogt, hid), (nmt, prg))):
        mlp_part[:, i * ff:(i + 1) * ff] = dot_nn(left[rows, done], right[done])
    other_cut_landed()
    last = slice(3 * tok, 4 * tok)
    mirror = []

    def finish(i, left, right):
        both = mlp_part[:, i * ff:(i + 1) * ff] + dot_nn(left[rows, last], right[last])
        mlp_part[:, i * ff:(i + 1) * ff] = both
        mlp_send[i, 0] = both[0:piece].astype(BF16)
        mlp_send[i, 1] = both[piece:span].astype(BF16)
        mirror.append(send(mlp_send.at[i, 1 - x], mlp_recv.at[i], x_peer))

    take(core_in[3, 0])
    value, slope = gelu_and_slope(dot_nn(nm[3], w_up[...]))
    hid[last] = value.astype(BF16)
    grad_h[...] = slope
    take(cut["core"])
    ogt[:, last] = og_cut[...].T
    finish(0, ogt, hid)
    nmt[:, last] = nm[3, :, window].T
    other_landed(3, 1)
    core2.wait_recv()
    sb2[...] = (mp2[c, 1 - y].astype(F32) + ra2[1 - y].astype(F32)).astype(BF16)
    y2 = send(sb2, rb2, y_peer)
    gv_cross = halve(gv_side, gv_part, gv_recv, gv_pass, gv_last)
    take(core_in[3, 1])
    prg[last] = (grad_h[...] * dot_nt(og[3], w_down[...])).astype(BF16)
    finish(1, nmt, prg)
    y2.wait_recv()
    grad = mp2[c, y].astype(F32) + ra2[y].astype(F32) + rb2[...].astype(F32)
    in_grad[...] = (mid_rows[y] + norm_back(inputs[mine].astype(F32), grad)).astype(BF16)
    stores = []

    def store(src, dst):
        one = pltpu.make_async_copy(src, dst, local_sem.at[8 + len(stores)])
        one.start()
        stores.append(one)

    own = pl.ds(pl.multiple_of(x * piece, piece), piece)
    store(in_grad, in_grad_h)
    for i in range(2):
        store(mlp_part.at[own, pl.ds(i * ff, ff)], mlp_own_h.at[i])
    go_cross.wait_recv()
    go_sum[...] = go_part[parity, upper] + go_recv[upper].astype(F32) + go_last[...].astype(F32)
    store(go_sum, go_sum_h)
    gv_cross.wait_recv()
    gv_sum[...] = gv_part[parity, upper] + gv_recv[upper].astype(F32) + gv_last[...].astype(F32)
    store(gv_sum, gv_sum_h)
    for one in stores:
        one.wait()
    for one in mirror:
        one.wait_recv()
    for one in started:
        one.wait_send()


def last_sums_kernel(
    in_grad, gv_sum, go_sum, mlp_own, mlp_recv, in_grad_h, gv_sum_h, go_sum_h, up_sum_h, down_sum_h, sums, sem
):
    stores = []

    def store(src, dst):
        one = pltpu.make_async_copy(src, dst, sem.at[len(stores)])
        one.start()
        stores.append(one)

    for i, dst in enumerate((down_sum_h, up_sum_h)):
        sums[i] = mlp_own[i] + mlp_recv[i].astype(F32)
        store(sums.at[i], dst)
    store(in_grad, in_grad_h)
    store(gv_sum, gv_sum_h)
    store(go_sum, go_sum_h)
    for one in stores:
        one.wait()


def on_device_fused(inputs, middle, out_grad, cached_maps, w_value, w_out, w_up, w_down):
    tok, width = inputs.shape
    local, ff = w_value.shape[1], w_up.shape[1]
    heads_here = cached_maps.shape[1]
    piece = width // lax.axis_size("img")
    share = tok // 4
    vmem = pl.BlockSpec(memory_space=pltpu.VMEM)
    anywhere = pl.BlockSpec(memory_space=pl.ANY)
    shape = jax.ShapeDtypeStruct
    results = (
        shape((share, width), BF16),
        shape((piece, local), F32),
        shape((piece, local), F32),
        shape((piece, ff), F32),
        shape((piece, ff), F32),
    )
    sums = pl.pallas_call(
        block_kernel,
        out_shape=results[:3] + (shape((2, piece, ff), F32), shape((2, piece, ff), BF16)),
        in_specs=[anywhere] * 8,
        out_specs=(anywhere,) * 5,
        scratch_shapes=[
            pltpu.VMEM((tok, width), BF16),
            pltpu.VMEM((tok, width), BF16),
            pltpu.VMEM((heads_here, tok, tok), BF16),
            pltpu.VMEM((local, width), BF16),
            pltpu.VMEM((local, width), BF16),
            pltpu.VMEM((width, ff), BF16),
            pltpu.VMEM((ff, width), BF16),
            pltpu.VMEM((4, tok, width), BF16),
            pltpu.VMEM((4, tok, width), BF16),
            pltpu.VMEM((tok, 384), BF16),
            pltpu.VMEM((384, 4 * tok), BF16),
            pltpu.VMEM((384, 4 * tok), BF16),
            pltpu.VMEM((4 * tok, ff), BF16),
            pltpu.VMEM((4 * tok, ff), BF16),
            pltpu.VMEM((tok, ff), F32),
            pltpu.VMEM((share, width), BF16),
            pltpu.VMEM((piece, local), F32),
            pltpu.VMEM((piece, local), F32),
            pltpu.VMEM((2 * piece, 2 * ff), F32),
            pltpu.VMEM((2, 2, piece, ff), BF16),
            pltpu.VMEM((2, 2, share, width), BF16),
            pltpu.VMEM((2, share, width), BF16),
            pltpu.VMEM((2, share, width), BF16),
            pltpu.VMEM((2, share, width), BF16),
            pltpu.VMEM((2, 2, share, width), BF16),
            pltpu.VMEM((2, share, width), BF16),
            pltpu.VMEM((share, width), BF16),
            pltpu.VMEM((share, width), BF16),
            pltpu.VMEM((2, share, width), F32),
            pltpu.VMEM((tok, width), BF16),
            pltpu.VMEM((2, 4, piece, tok), BF16),
            pltpu.VMEM((4, piece, tok), BF16),
            pltpu.VMEM((2, 4, piece, tok), BF16),
            pltpu.VMEM((4, piece, tok), BF16),
            pltpu.VMEM((tok, local), BF16),
            pltpu.VMEM((tok, local), BF16),
            pltpu.VMEM((tok, local), BF16),
            pltpu.VMEM((tok, local), BF16),
        ] + [
            pltpu.VMEM((2, 2, piece, local), F32),
            pltpu.VMEM((2, 2, piece, local), BF16),
            pltpu.VMEM((2, piece, local), BF16),
            pltpu.VMEM((piece, local), BF16),
            pltpu.VMEM((piece, local), BF16),
        ] * 2 + [
            pltpu.SemaphoreType.DMA((13,)),
            pltpu.SemaphoreType.DMA((COPIES,)),
            pltpu.SemaphoreType.DMA((COPIES,)),
        ],
        compiler_params=pltpu.CompilerParams(
            collective_id=0, has_side_effects=True, vmem_limit_bytes=56 * 1024 * 1024
        ),
    )(inputs, middle, out_grad, cached_maps[0], w_value.T, w_out, w_up, w_down)
    in_grad, value_rows, out_rows_t, up_rows, down_rows_t = pl.pallas_call(
        last_sums_kernel,
        out_shape=results,
        in_specs=[vmem] * 5,
        out_specs=(anywhere,) * 5,
        scratch_shapes=[pltpu.VMEM((2, piece, ff), F32), pltpu.SemaphoreType.DMA((5,))],
    )(*sums)
    return in_grad, value_rows, out_rows_t.T, up_rows, down_rows_t.T


def solution(mesh):
    fused = mesh.shape["img"] == 8 and mesh.shape["head"] == 4
    return jax.shard_map(
        on_device_fused if fused else on_device,
        mesh=mesh,
        in_specs=(
            P("img", None),
            P("img", None),
            P("img", None),
            P("img", "head", None, None),
            P(None, "head"),
            P("head", None),
            P(None, "head"),
            P("head", None),
        ),
        out_specs=(
            P(("img", "head"), None),
            P("img", "head"),
            P("head", "img"),
            P("img", "head"),
            P("head", "img"),
        ),
        check_vma=False,
    )
```
